512 devices in a mesh: dp: 16 (over x, y), expert: 32 (over z, core).
Axes of the slice: x: 4, y: 4, z: 16, core: 2. Of those that a mesh axis runs over, the one named last changes fastest.
Arguments:
- tokens: bfloat16 [65536, 3584], P(('dp', 'expert')), may hold values from -6 to 6
- cotangent: bfloat16 [65536, 3584], P(('dp', 'expert')), may hold values from -6 to 6
- route_weight: float32 [65536, 8], P(('dp', 'expert')), may hold values from 0.05 to 0.5
- expert_ids: int32 [65536, 8], P(('dp', 'expert')), may hold values from 0 to 255, as said below
- live_tokens: int32 [512], P(('dp', 'expert')), may hold values from 1 to 128, 49152 in all
- replica_plan: int32 [512, 4], P(('dp', 'expert')), may hold values 0 or 1
- w_gate: bfloat16 [3584, 8192], P('dp', 'expert'), may hold values from -0.09375 to 0.09375
- w_up: bfloat16 [3584, 8192], P('dp', 'expert'), may hold values from -0.09375 to 0.09375
- w_down: bfloat16 [8192, 3584], P('expert', 'dp'), may hold values from -0.125 to 0.125
- scale_gate: float32 [28, 64], P(None, 'expert'), may hold values from 0.5 to 2
- scale_up: float32 [28, 64], P(None, 'expert'), may hold values from 0.5 to 2
- scale_down: float32 [64, 28], P('expert'), may hold values from 0.5 to 2
Outputs:
- d_tokens: bfloat16 [65536, 3584], P(('dp', 'expert'))
- grad_gate: bfloat16 [3584, 8192], P('dp', 'expert')
- grad_up: bfloat16 [3584, 8192], P('dp', 'expert')
- grad_down: bfloat16 [8192, 3584], P('expert', 'dp')
The draws below stay inside these ranges and needn't reach their ends.
Inputs may be any that keep to these rules, and one draw needn't show every extreme that they name: `expert_ids`: the 8 ids of one token are distinct.
All inputs are finite; a program needn't handle non-finite values. No bound on the sum of `live_tokens` or of `replica_plan` on one device may be relied on, other than what follows from the above.
Results may differ from the reference program's by a relative error of at most 0.012.
Values may be sent and summed in bfloat16 or wider, within the bound.
A program may use at most 64 MiB of HBM per device.

```python
import math
import jax
import jax.numpy as jnp
import numpy as np
from jax import lax

D = 3584
EXP_HID = 2048
EXPERTS_ALL = 256
TOPK = 8
HSH = 8
BLOCK = 128
TOK_DEV = 128
CAP = 4
HID = 256
EXPERTS = 4
TOKENS = 65536
N_DP = 16
N_EXPERT = 32


def draw_expert_ids(key, part):
    key_select, key_busiest, key_offset = jax.random.split(key, 3)
    outside_count = EXPERTS_ALL - EXPERTS
    selector = jax.random.randint(key_select, (TOKENS,), 0, TOK_DEV // CAP)
    busiest = jax.random.randint(key_busiest, (), 0, EXPERTS)
    offset_draw = jax.random.randint(key_offset, (TOKENS,), 0, outside_count)
    outside = EXPERTS + (offset_draw[:, None] + jnp.arange(TOPK, dtype=jnp.int32)[None, :]) % outside_count
    leading = jnp.where(selector < EXPERTS, selector, jnp.where(selector < 2 * EXPERTS, busiest, outside[:, TOPK - 1]))
    return jnp.concatenate([leading[:, None], outside[:, :TOPK - 1]], axis=1).astype(jnp.int32)


def touch_ends(array, key, least, high):
    longest = array.shape.index(max(array.shape))
    spots = []
    for shift in (0, 1):
        where = [jax.random.randint(jax.random.fold_in(key, axis), (), 0, length) for axis, length in enumerate(array.shape)]
        where[longest] = (where[longest] + shift) % array.shape[longest]
        spots.append(tuple(where))
    return array.at[spots[0]].set(least).at[spots[1]].set(high)


def levels(own_key, shape, pieces, least, largest):
    factor_of, own = 1.0, jax.random.fold_in(own_key, 6)
    for dim, shards_of in pieces:
        heights = jnp.exp(jax.random.uniform(jax.random.fold_in(own, dim), (shards_of,), jnp.float32, least / len(pieces), largest / len(pieces)))
        factor_of = factor_of * jnp.repeat(heights, shape[dim] // shards_of).reshape([-1 if axis == dim else 1 for axis in range(len(shape))])
    return factor_of


def profile(amount, total, bound, lean):
    portions = [(1 << 20) // math.isqrt(standing ** lean) + 1 for standing in range(2, amount + 1)]
    rest, given = total - bound - (amount - 1), [1] * (amount - 1)
    while rest > 0:
        movable = [i for i in range(amount - 1) if given[i] < bound]
        mass, budget = sum([portions[i] for i in movable]), rest
        for i in movable:
            more = min(bound - given[i], max(1, budget * portions[i] // mass), rest)
            given[i] = given[i] + more
            rest = rest - more
    return np.array([bound] + given)


def uneven_parts(stream_key, number_of, total, reach, skew):
    if number_of == 2:
        one = jax.random.randint(stream_key, (), max(1, total - reach), min(reach, total - 1) + 1)
        return jnp.stack([one, total - one])
    sizes = jnp.asarray(profile(number_of, total, reach, skew), jnp.int32)
    pairs = (number_of - 1) // 2
    donor, sink = sizes[1:1 + 2 * pairs:2], sizes[2:2 + 2 * pairs:2]
    room = jnp.minimum(donor - 1, reach - sink)
    shifted = jax.random.randint(jax.random.fold_in(stream_key, 1), (pairs,), 0, 1 << 20) % (room + 1)
    sizes = sizes.at[1:1 + 2 * pairs:2].set(donor - shifted).at[2:2 + 2 * pairs:2].set(sink + shifted)
    return sizes[jax.random.permutation(jax.random.fold_in(stream_key, 2), number_of)]


def scatter_about(own_key, shape, scale, limit, cuts=(), kind=jnp.bfloat16):
    values = jax.random.normal(own_key, shape, jnp.float32) * scale
    if len(cuts) > 0:
        values = levels(own_key, shape, cuts, -0.22, 0.18) * values
    return jnp.clip(values, min=-limit, max=limit).astype(kind)


def setup_inputs(seed: int = 0) -> dict:
    key_list = jax.random.split(jax.random.key(seed), 13)
    tokens = scatter_about(key_list[0], (TOKENS, D), 1.0, 6.0, ((0, 512),))
    cotangent = scatter_about(key_list[1], (TOKENS, D), 1.0, 6.0, ((0, 512),))
    route_weight = jnp.clip(jnp.exp(math.log(0.5) - 2.3025851 * jax.random.uniform(key_list[2], (TOKENS, TOPK), jnp.float32) ** levels(key_list[2], (TOKENS, TOPK), ((0, 512),), -0.2, 0.2)), 0.05, 0.5)
    expert_ids = draw_expert_ids(jax.random.fold_in(key_list[12], 71), 0)
    live_tokens = uneven_parts(key_list[4], N_DP * N_EXPERT, N_DP * N_EXPERT * TOK_DEV * 3 // 4, TOK_DEV, 0).astype(jnp.int32)
    replica_plan = touch_ends((jax.random.randint(key_list[5], (N_DP * N_EXPERT, EXPERTS), 0, 2) < 1).astype(jnp.int32), jax.random.fold_in(key_list[5], 1), 0, 1)
    w_gate = scatter_about(key_list[6], (D, N_EXPERT * HID), D ** -0.5, 0.09375, ((0, 16), (1, 32)))
    w_up = scatter_about(key_list[7], (D, N_EXPERT * HID), D ** -0.5, 0.09375, ((0, 16), (1, 32)))
    w_down = scatter_about(key_list[8], (N_EXPERT * HID, D), EXP_HID ** -0.5, 0.125, ((0, 32), (1, 16)))
    scale_gate = jnp.clip(jnp.exp(math.log(2.0) - 1.3862944 * jax.random.uniform(key_list[9], (D // BLOCK, N_EXPERT * HID // BLOCK), jnp.float32) ** levels(key_list[9], (D // BLOCK, N_EXPERT * HID // BLOCK), ((1, 32),), -0.2, 0.2)), 0.5, 2.0)
    scale_up = jnp.clip(jnp.exp(math.log(2.0) - 1.3862944 * jax.random.uniform(key_list[10], (D // BLOCK, N_EXPERT * HID // BLOCK), jnp.float32) ** levels(key_list[10], (D // BLOCK, N_EXPERT * HID // BLOCK), ((1, 32),), -0.2, 0.2)), 0.5, 2.0)
    scale_down = jnp.clip(jnp.exp(math.log(2.0) - 1.3862944 * jax.random.uniform(key_list[11], (N_EXPERT * HID // BLOCK, D // BLOCK), jnp.float32) ** levels(key_list[11], (N_EXPERT * HID // BLOCK, D // BLOCK), ((0, 32),), -0.2, 0.2)), 0.5, 2.0)
    return dict(tokens=tokens, cotangent=cotangent, route_weight=route_weight, expert_ids=expert_ids, live_tokens=live_tokens, replica_plan=replica_plan, w_gate=w_gate, w_up=w_up, w_down=w_down, scale_gate=scale_gate, scale_up=scale_up, scale_down=scale_down)


def dequantize(values, scale):
    block_rows = values.shape[0] // scale.shape[0]
    block_cols = values.shape[1] // scale.shape[1]
    spread = jnp.repeat(jnp.repeat(scale, block_rows, axis=0), block_cols, axis=1)
    return (values.astype(jnp.float32) * spread).astype(jnp.bfloat16)


def route_rows(tokens, cotangent, route_weight, expert_ids, live_count, plan, experts, capacity):
    count = tokens.shape[0]
    token_index = jnp.arange(count, dtype=jnp.int32)
    expert_index = jnp.arange(experts, dtype=jnp.int32)
    matches = expert_ids[:, None, :] == expert_index[None, :, None]
    routed = jnp.any(matches, axis=2) & (token_index < live_count)[:, None]
    to_replica = ((token_index % 2) == 1)[:, None] & (plan[None, :] == 1)
    in_lists = jnp.stack([routed & (~to_replica), routed & to_replica], axis=2).astype(jnp.int32)
    position = jnp.cumsum(in_lists, axis=0) - 1
    capacity_index = jnp.arange(capacity, dtype=jnp.int32)
    selected = ((in_lists[..., None] == 1) & (position[..., None] == capacity_index)).astype(jnp.float32)
    weight_sum = jnp.sum(jnp.where(matches, route_weight[:, None, :], jnp.float32(0.0)), axis=2)
    row_weight = jnp.sum(selected * weight_sum[:, :, None, None], axis=0)
    flat = selected.reshape(count, -1)
    picker = flat.T.astype(jnp.bfloat16)
    token_rows = jnp.dot(picker, tokens, preferred_element_type=jnp.float32).astype(jnp.bfloat16)
    cot_picked = jnp.dot(picker, cotangent, preferred_element_type=jnp.float32)
    cot_rows = (row_weight.reshape(-1, 1) * cot_picked).astype(jnp.bfloat16)
    shape = (experts, 2, capacity, tokens.shape[1])
    return flat, token_rows.reshape(shape), cot_rows.reshape(shape)


def expert_terms(token_rows, cot_rows, gate_w, up_w, down_w, shards):
    gate_pre = jnp.dot(token_rows, gate_w, preferred_element_type=jnp.float32)
    up_pre = jnp.dot(token_rows, up_w, preferred_element_type=jnp.float32)
    gate_sig = jax.nn.sigmoid(gate_pre)
    swish = gate_pre * gate_sig
    d_hidden = jnp.dot(cot_rows, down_w.T, preferred_element_type=jnp.float32)
    hidden = (swish * up_pre).astype(jnp.bfloat16)
    d_up = (d_hidden * swish).astype(jnp.bfloat16)
    d_gate = (d_hidden * up_pre * gate_sig * (1.0 + gate_pre * (1.0 - gate_sig))).astype(jnp.bfloat16)
    grad_g = jnp.dot(token_rows.T, d_gate, preferred_element_type=jnp.float32).astype(jnp.bfloat16)
    grad_u = jnp.dot(token_rows.T, d_up, preferred_element_type=jnp.float32).astype(jnp.bfloat16)
    grad_d = jnp.dot(hidden.T, cot_rows, preferred_element_type=jnp.float32).astype(jnp.bfloat16)
    rows = token_rows.shape[0]
    width = token_rows.shape[1]
    gate_parts = jnp.einsum("rkh,dkh->krd", d_gate.astype(jnp.float32).reshape(rows, shards, -1),
                            gate_w.astype(jnp.float32).reshape(width, shards, -1), precision=lax.Precision.HIGHEST)
    up_parts = jnp.einsum("rkh,dkh->krd", d_up.astype(jnp.float32).reshape(rows, shards, -1),
                          up_w.astype(jnp.float32).reshape(width, shards, -1), precision=lax.Precision.HIGHEST)
    parts = (gate_parts + up_parts).astype(jnp.bfloat16).astype(jnp.float32)
    return grad_g, grad_u, grad_d, jnp.sum(parts, axis=0)


def reference(tokens, cotangent, route_weight, expert_ids, live_tokens, replica_plan, w_gate, w_up, w_down,
              scale_gate, scale_up, scale_down):
    devices = N_DP * N_EXPERT
    width = tokens.shape[1]

    def per_device(tok_block, cot_block, weight_block, id_block, live_count, plan_row):
        return route_rows(tok_block, cot_block, weight_block, id_block, live_count, plan_row, EXPERTS, CAP)

    flat, token_rows, cot_rows = jax.vmap(per_device)(
        tokens.reshape(devices, TOK_DEV, width), cotangent.reshape(devices, TOK_DEV, width),
        route_weight.reshape(devices, TOK_DEV, TOPK), expert_ids.reshape(devices, TOK_DEV, TOPK), live_tokens,
        replica_plan)
    token_rows = token_rows.reshape(N_DP, N_EXPERT, EXPERTS, 2, CAP, width)
    cot_rows = cot_rows.reshape(N_DP, N_EXPERT, EXPERTS, 2, CAP, width)
    gate_all = dequantize(w_gate, scale_gate)
    up_all = dequantize(w_up, scale_up)
    down_all = dequantize(w_down, scale_down)
    gate_list, up_list, down_list, row_list = [], [], [], []
    for expert in range(EXPERTS):
        start = expert * EXP_HID
        gate_w = gate_all[:, start:start + EXP_HID]
        up_w = up_all[:, start:start + EXP_HID]
        down_w = down_all[start:start + EXP_HID, :]

        def group(pair):
            rows_x, rows_c = pair
            leading = expert_terms(rows_x[:, 0].reshape(-1, width), rows_c[:, 0].reshape(-1, width),
                                   gate_w, up_w, down_w, HSH)
            trailing = expert_terms(rows_x[:, 1].reshape(-1, width), rows_c[:, 1].reshape(-1, width),
                                    gate_w, up_w, down_w, HSH)
            sum_gate = (leading[0].astype(jnp.float32) + trailing[0].astype(jnp.float32)).astype(jnp.bfloat16)
            sum_up = (leading[1].astype(jnp.float32) + trailing[1].astype(jnp.float32)).astype(jnp.bfloat16)
            sum_down = (leading[2].astype(jnp.float32) + trailing[2].astype(jnp.float32)).astype(jnp.bfloat16)
            dx_rows = jnp.stack([leading[3].reshape(N_EXPERT, CAP, width),
                                 trailing[3].reshape(N_EXPERT, CAP, width)], axis=1)
            return sum_gate, sum_up, sum_down, dx_rows

        result = lax.map(group, (token_rows[:, :, expert], cot_rows[:, :, expert]))
        gate_list.append(jnp.sum(result[0].astype(jnp.float32), axis=0).astype(jnp.bfloat16))
        up_list.append(jnp.sum(result[1].astype(jnp.float32), axis=0).astype(jnp.bfloat16))
        down_list.append(jnp.sum(result[2].astype(jnp.float32), axis=0).astype(jnp.bfloat16))
        row_list.append(result[3])
    dx_rows = jnp.stack(row_list, axis=2).reshape(devices, -1, width)

    def gather_back(selection, rows):
        return jnp.dot(selection, rows, precision=lax.Precision.HIGHEST)

    d_tokens = jax.vmap(gather_back)(flat, dx_rows).astype(jnp.bfloat16).reshape(TOKENS, width)
    grad_gate = jnp.concatenate(gate_list, axis=1)
    grad_up = jnp.concatenate(up_list, axis=1)
    grad_down = jnp.concatenate(down_list, axis=0)
    return (d_tokens, grad_gate, grad_up, grad_down)
```

```python
import functools

import jax
import jax.numpy as jnp
from jax import lax
from jax.experimental import pallas as pl
from jax.experimental.pallas import tpu as pltpu
from jax.sharding import PartitionSpec as P

HSH = 8
CAP = 4
BLOCK = 128
MESH = pl.DeviceIdType.MESH

NX = 4
NZ = 16
SEG = 4
ROWS = 2 * CAP

HALF = ((0, 112), (112, 112))
PART = (((0, 64), (64, 48)), ((112, 48), (160, 64)))

HOPS = 10
STEPS = tuple((h, r) for h in range(HOPS) for r in (2, 1, 0))


def passes_on(h, r, q):
    d = (h + 3 - q) // 4
    p = (q - h) % 4
    if r == 0:
        return d == 0 and q < 3
    if r == 1:
        return d == 0 or (d == 1 and q < 3)
    return p >= 2 and (d <= 1 or (d == 2 and q < 3))


def onward(h, r):
    return tuple(q for q in range(4) if passes_on(h, r, q))


def arrives(h, r):
    return tuple(q for q in range(4) if h > 0 and passes_on(h - 1, r, (q - 1) % 4))


def kept(h, r):
    return tuple(q for q in arrives(h, r) if (h + 3 - q) // 4 == r)


def when_in(q, places, body):
    if not places:
        return
    if len(places) == 4:
        body()
        return
    test = q == places[0]
    for place in places[1:]:
        test = test | (q == place)
    pl.when(test)(body)


def place_of():
    g = lax.axis_index("dp")
    j = lax.axis_index("expert")
    return g // NX, g % NX, j // 2, j % 2


def greet(neighbours):
    barrier = pltpu.get_barrier_semaphore()
    for device in neighbours:
        pl.semaphore_signal(barrier, inc=1, device_id=device, device_id_type=MESH)
    pl.semaphore_wait(barrier, len(neighbours))


def at_offset(x, y, axis, offset):
    if axis == 0:
        return ((x + offset) % NX) * NX + y
    return x * NX + (y + offset) % NX


def block_at(x, y, half, i, k):
    if half == 0:
        return ((x + i) % NX) * NX + (y + k) % NX
    return ((x + k) % NX) * NX + (y + i) % NX


def remote(src, dst, send, recv, device):
    return pltpu.make_async_remote_copy(
        src_ref=src,
        dst_ref=dst,
        send_sem=send,
        recv_sem=recv,
        device_id=device,
        device_id_type=MESH,
    )


def gather_kernel(
    w_ref, rows_ref, full_ref, u_ref, w_send, w_recv, z_send, z_recv, p_send, p_recv, own_sem
):
    x, y, z, c = place_of()
    g = x * NX + y
    j = z * 2 + c
    seg = z // SEG
    partner = (g, z * 2 + 1 - c)

    def across(axis, way):
        return (at_offset(x, y, axis, way), j)

    def along(way):
        return (g, ((z + way + NZ) % NZ) * 2 + c)

    greet(
        [across(0, 1), across(0, -1), across(1, 1), across(1, -1), along(1), along(-1), partner]
    )

    keep_w = pltpu.make_async_copy(w_ref, full_ref.at[:, g], own_sem.at[0])
    keep_rows = pltpu.make_async_copy(rows_ref.at[seg], u_ref.at[seg, :, z, c], own_sem.at[1])

    def place(way):
        q = z % SEG
        return q if way == 1 else SEG - 1 - q

    def row_block(way, h, r):
        s = (z - way * h + NZ) % NZ
        e = (s // SEG + way * r + SEG) % SEG
        return s, e

    def row_copy(way, h, r):
        n = 0 if way == 1 else 1
        s, e = row_block(way, h, r)
        src = rows_ref.at[e] if h == 0 else u_ref.at[e, :, s, c]
        return remote(
            src, u_ref.at[e, :, s, c], z_send.at[n, h, r], z_recv.at[n, h + 1, r], along(way)
        )

    def row_arrival(way, h, r):
        n = 0 if way == 1 else 1
        s, e = row_block(way, h, r)
        slot = u_ref.at[e, :, s, c]
        return remote(slot, slot, z_send.at[n, h, r], z_recv.at[n, h, r], along(way))

    def share(way, h):
        n = 0 if way == 1 else 1
        s = (z - way * h + NZ) % NZ
        slot = u_ref.at[seg, :, s, c]
        src = rows_ref.at[seg] if h == 0 else slot
        return remote(src, slot, p_send.at[n, h], p_recv.at[n, h], partner)

    def shared(way, h):
        n = 0 if way == 1 else 1
        s = (z - way * h + NZ) % NZ
        slot = u_ref.at[seg, :, s, 1 - c]
        return remote(slot, slot, p_send.at[n, h], p_recv.at[n, h], partner)

    def row_step(h):
        for r in (2, 1, 0):
            for way in (1, -1):
                q = place(way)
                when_in(q, arrives(h, r), lambda way=way, r=r: row_arrival(way, h, r).wait_recv())
                when_in(q, onward(h, r), lambda way=way, r=r: row_copy(way, h, r).start())
                when_in(q, kept(h, r), lambda way=way: share(way, h).start())

    def w_copy(half, stage, way, part):
        first, second = (0, 1) if half == 0 else (1, 0)
        axis = first if stage == 0 else second
        i = 0 if stage == 0 else (0, 1, -1, 2)[stage - 1]
        if part is None:
            start, size = HALF[half]
            back = 0
        else:
            start, size = PART[half][part]
            back = -way
        if stage == 0:
            owner = block_at(x, y, half, back, 0)
        else:
            owner = block_at(x, y, half, i, back)
        slot = full_ref.at[:, owner, pl.ds(start, size)]
        own = part is None and (stage == 0 or i == 0)
        src = w_ref.at[:, pl.ds(start, size)] if own else slot
        n = 2 * (0 if part is None else 1) + (0 if way == 1 else 1)
        return remote(
            src, slot, w_send.at[half, stage, n], w_recv.at[half, stage, n], across(axis, way)
        )

    def w_arrival(half, stage, way, part):
        first, second = (0, 1) if half == 0 else (1, 0)
        axis = first if stage == 0 else second
        i = 0 if stage == 0 else (0, 1, -1, 2)[stage - 1]
        start, size = HALF[half] if part is None else PART[half][part]
        back = -way if part is None else -2 * way
        owner = block_at(x, y, half, back, 0) if stage == 0 else block_at(x, y, half, i, back)
        slot = full_ref.at[:, owner, pl.ds(start, size)]
        n = 2 * (0 if part is None else 1) + (0 if way == 1 else 1)
        return remote(
            slot, slot, w_send.at[half, stage, n], w_recv.at[half, stage, n], across(axis, way)
        )

    def w_start(stage):
        for half in (0, 1):
            for way in (1, -1):
                w_copy(half, stage, way, None).start()

    def w_forward(stage, then=None):
        for way in (1, -1):
            for half in (0, 1):
                w_arrival(half, stage, way, None).wait_recv()
                w_copy(half, stage, way, 0 if way == 1 else 1).start()
                if then is not None:
                    for other in (1, -1):
                        w_copy(half, then[way], other, None).start()

    row_step(0)
    w_start(0)
    w_start(1)
    share(1, 0).start()
    keep_w.start()
    keep_rows.start()
    row_step(1)
    w_forward(0, {1: 3, -1: 2})
    row_step(2)
    w_forward(1)
    for half in (0, 1):
        for way in (1, -1):
            w_arrival(half, 0, way, 0 if way == 1 else 1).wait_recv()
    w_start(4)
    row_step(3)
    w_forward(3)
    row_step(4)
    w_forward(2)
    row_step(5)
    w_forward(4)
    for h in range(6, HOPS):
        row_step(h)

    for stage in range(5):
        for half in (0, 1):
            for way in (1, -1):
                part = 0 if way == 1 else 1
                if stage > 0:
                    w_arrival(half, stage, way, part).wait_recv()
                w_copy(half, stage, way, None).wait_send()
                w_copy(half, stage, way, part).wait_send()
    share(1, 0).wait_send()
    shared(1, 0).wait_recv()
    for h in range(HOPS):
        for way in (1, -1):
            q = place(way)
            for r in (2, 1, 0):
                when_in(q, onward(h, r), lambda way=way, r=r: row_copy(way, h, r).wait_send())

                def end_share(way=way):
                    share(way, h).wait_send()
                    shared(way, h).wait_recv()

                when_in(q, kept(h, r), end_share)
    keep_w.wait()
    keep_rows.wait()


def gather(weights, rows):
    kinds, depth, hidden = weights.shape
    experts, streams, count, width = rows.shape
    dma = pltpu.SemaphoreType.DMA
    return pl.pallas_call(
        gather_kernel,
        out_shape=(
            jax.ShapeDtypeStruct((kinds, NX * NX, depth, hidden), jnp.bfloat16),
            jax.ShapeDtypeStruct((experts, streams, NZ, 2, count, width), jnp.bfloat16),
        ),
        in_specs=[pl.BlockSpec(memory_space=pl.ANY)] * 2,
        out_specs=(pl.BlockSpec(memory_space=pl.ANY),) * 2,
        scratch_shapes=[
            dma((2, 5, 4)),
            dma((2, 5, 4)),
            dma((2, HOPS + 1, 3)),
            dma((2, HOPS + 1, 3)),
            dma((2, HOPS)),
            dma((2, HOPS)),
            dma((2,)),
        ],
        compiler_params=pltpu.CompilerParams(collective_id=0, has_side_effects=True),
    )(weights, rows)


def reduce_kernel(
    g_ref,
    dx_ref,
    grad_ref,
    out_ref,
    v_part,
    v_whole,
    theirs,
    total,
    held,
    v_send,
    v_recv,
    z_send,
    z_recv,
    p_sem,
):
    x, y, z, c = place_of()
    g = x * NX + y
    j = z * 2 + c
    seg = z // SEG
    partner = (g, z * 2 + 1 - c)

    def across(axis, way):
        return (at_offset(x, y, axis, way), j)

    def along(way):
        return (g, ((z + way + NZ) % NZ) * 2 + c)

    greet(
        [across(0, 1), across(0, -1), across(1, 1), across(1, -1), along(1), along(-1), partner]
    )

    swap = remote(dx_ref.at[:, 1 - c], theirs, p_sem.at[0], p_sem.at[1], partner)
    swap.start()

    f32 = jnp.float32

    def owner_of(half, stage, back):
        i = 0 if stage == 0 else (0, 1, -1, 2)[stage - 1]
        if stage == 0:
            return block_at(x, y, half, back, 0)
        return block_at(x, y, half, i, back)

    def axis_of(half, stage):
        first, second = (0, 1) if half == 0 else (1, 0)
        return first if stage == 0 else second

    def g_part(half, stage, way):
        k = 0 if way == 1 else 1
        start, size = PART[half][k]
        return remote(
            g_ref.at[:, owner_of(half, stage, 2), pl.ds(start, size)],
            v_part.at[half, stage, k, :, pl.ds(0, size)],
            v_send.at[half, stage, k],
            v_recv.at[half, stage, k],
            across(axis_of(half, stage), way),
        )

    def g_whole(half, stage, way):
        k = 0 if way == 1 else 1
        start, size = HALF[half]
        return remote(
            g_ref.at[:, owner_of(half, stage, way), pl.ds(start, size)],
            v_whole.at[half, stage, k],
            v_send.at[half, stage, 2 + k],
            v_recv.at[half, stage, 2 + k],
            across(axis_of(half, stage), way),
        )

    def parts_out(stage):
        for half in (0, 1):
            for way in (1, -1):
                g_part(half, stage, way).start()

    def parts_in(stage):
        for half in (0, 1):
            for way in (1, -1):
                k = 0 if way == 1 else 1
                start, size = PART[half][k]
                g_part(half, stage, way).wait_recv()
                block = owner_of(half, stage, way)

                def add(m, _, half=half, k=k, start=start, size=size, block=block):
                    here = g_ref[m, block, pl.ds(start, size), :].astype(f32)
                    came = v_part[half, stage, k, m, pl.ds(0, size), :].astype(f32)
                    g_ref[m, block, pl.ds(start, size), :] = (here + came).astype(jnp.bfloat16)
                    return 0

                lax.fori_loop(0, 3, add, 0)
                g_whole(half, stage, way).start()

    def wholes_in(stage):
        for half in (0, 1):
            start, size = HALF[half]
            g_whole(half, stage, 1).wait_recv()
            g_whole(half, stage, -1).wait_recv()
            block = owner_of(half, stage, 0)

            def add(m, _, half=half, start=start, size=size, block=block):
                here = g_ref[m, block, pl.ds(start, size), :].astype(f32)
                one = v_whole[half, stage, 0, m].astype(f32)
                two = v_whole[half, stage, 1, m].astype(f32)
                summed = (here + one + two).astype(jnp.bfloat16)
                if stage == 0:
                    grad_ref[m, pl.ds(start, size), :] = summed
                else:
                    g_ref[m, block, pl.ds(start, size), :] = summed
                return 0

            lax.fori_loop(0, 3, add, 0)

    def place(way):
        q = z % SEG
        return q if way == 1 else SEG - 1 - q

    def back_copy(way, h, r, fresh):
        n = 0 if way == 1 else 1
        s = (z - way * h + NZ) % NZ
        src = total.at[s] if fresh else held.at[n, h, r]
        return remote(
            src, held.at[n, h - 1, r], z_send.at[n, h, r], z_recv.at[n, h - 1, r], along(-way)
        )

    def back_arrival(way, h, r):
        n = 0 if way == 1 else 1
        slot = held.at[n, h, r]
        return remote(slot, slot, z_send.at[n, h, r], z_recv.at[n, h, r], along(way))

    def back_step(h):
        for r in (2, 1, 0):
            for way in (1, -1):
                n = 0 if way == 1 else 1
                q = place(way)
                s = (z - way * h + NZ) % NZ
                more, come, own = onward(h, r), arrives(h, r), kept(h, r)
                last = tuple(p for p in come if p not in more)
                relay = tuple(p for p in come if p in more and p not in own)
                joined = tuple(p for p in come if p in more and p in own)

                def start_last(way=way, r=r):
                    back_copy(way, h, r, True).start()

                def start_relay(way=way, r=r):
                    back_arrival(way, h, r).wait_recv()
                    back_copy(way, h, r, False).start()

                def start_joined(way=way, r=r, n=n, s=s):
                    back_arrival(way, h, r).wait_recv()
                    held[n, h, r] = (held[n, h, r].astype(f32) + total[s].astype(f32)).astype(
                        jnp.bfloat16
                    )
                    back_copy(way, h, r, False).start()

                when_in(q, last, start_last)
                when_in(q, relay, start_relay)
                when_in(q, joined, start_joined)

    parts_out(4)
    parts_out(2)
    parts_out(3)
    parts_out(1)
    swap.wait()

    def own_total(s, _):
        total[s] = (dx_ref[s, c].astype(f32) + theirs[s].astype(f32)).astype(jnp.bfloat16)
        return 0

    lax.fori_loop(0, NZ, own_total, 0)
    back_step(9)
    back_step(8)
    parts_in(4)
    back_step(7)
    parts_in(2)
    back_step(6)
    parts_in(3)
    back_step(5)
    parts_in(1)
    back_step(4)
    wholes_in(4)
    parts_out(0)
    back_step(3)
    wholes_in(2)
    wholes_in(3)
    back_step(2)
    parts_in(0)
    back_step(1)
    wholes_in(1)

    q = z % SEG
    out_ref[seg] = total[z]

    def take(n, r):
        way = 1 if n == 0 else -1
        e = (seg + way * r + SEG) % SEG
        back_arrival(way, 0, r).wait_recv()
        if r == 0:
            out_ref[seg] = (out_ref[seg].astype(f32) + held[n, 0, 0].astype(f32)).astype(
                jnp.bfloat16
            )
        else:
            out_ref[e] = held[n, 0, r]

    for n in (0, 1):
        for r in (1, 2, 0):
            when_in(place(1 if n == 0 else -1), onward(0, r), functools.partial(take, n, r))

    wholes_in(0)

    for stage in range(5):
        for half in (0, 1):
            for way in (1, -1):
                g_part(half, stage, way).wait_send()
                g_whole(half, stage, way).wait_send()
    for h, r in STEPS:
        for way in (1, -1):
            when_in(
                place(way),
                arrives(h, r),
                lambda way=way, h=h, r=r: back_copy(way, h, r, False).wait_send(),
            )


def reduce_back(terms, dx):
    kinds, groups, depth, hidden = terms.shape
    count, width = dx.shape[2:]
    dma = pltpu.SemaphoreType.DMA
    vmem = pltpu.VMEM
    bf16 = jnp.bfloat16

    return pl.pallas_call(
        reduce_body,
        out_shape=(
            jax.ShapeDtypeStruct((kinds, depth, hidden), bf16),
            jax.ShapeDtypeStruct((SEG, count, width), bf16),
        ),
        in_specs=[
            pl.BlockSpec(memory_space=pl.ANY),
            pl.BlockSpec(memory_space=pltpu.VMEM),
        ],
        out_specs=(pl.BlockSpec(memory_space=pltpu.VMEM),) * 2,
        scratch_shapes=[
            vmem((kinds, groups, depth, hidden), bf16),
            vmem((2, 5, 2, kinds, 64, hidden), bf16),
            vmem((2, 5, 2, kinds, 112, hidden), bf16),
            vmem((NZ, count, width), bf16),
            vmem((NZ, count, width), bf16),
            vmem((2, HOPS, 3, count, width), bf16),
            dma((2, 5, 4)),
            dma((2, 5, 4)),
            dma((2, HOPS, 3)),
            dma((2, HOPS, 3)),
            dma((2,)),
            dma((1,)),
        ],
        compiler_params=pltpu.CompilerParams(collective_id=1, has_side_effects=True),
    )(terms, dx)


def reduce_body(g_in, dx_ref, grad_ref, out_ref, g_ref, *rest):
    load = pltpu.make_async_copy(g_in, g_ref, rest[-1].at[0])
    load.start()
    load.wait()
    reduce_kernel(g_ref, dx_ref, grad_ref, out_ref, *rest[:-1])


def route_rows(tokens, cotangent, route_weight, expert_ids, live_count, plan, experts, capacity):
    count = tokens.shape[0]
    token_index = jnp.arange(count, dtype=jnp.int32)
    expert_index = jnp.arange(experts, dtype=jnp.int32)
    matches = expert_ids[:, None, :] == expert_index[None, :, None]
    routed = jnp.any(matches, axis=2) & (token_index < live_count)[:, None]
    to_replica = (token_index % 2 == 1)[:, None] & (plan[None, :] == 1)
    in_lists = jnp.stack([routed & ~to_replica, routed & to_replica], axis=2).astype(jnp.int32)
    position = jnp.cumsum(in_lists, axis=0) - 1
    capacity_index = jnp.arange(capacity, dtype=jnp.int32)
    selected = ((in_lists[..., None] == 1) & (position[..., None] == capacity_index)).astype(
        jnp.float32
    )
    weight_sum = jnp.sum(jnp.where(matches, route_weight[:, None, :], jnp.float32(0.0)), axis=2)
    row_weight = jnp.sum(selected * weight_sum[:, :, None, None], axis=0)
    flat = selected.reshape(count, -1)
    picker = flat.T.astype(jnp.bfloat16)
    token_rows = jnp.dot(picker, tokens, preferred_element_type=jnp.float32).astype(jnp.bfloat16)
    cot_picked = jnp.dot(picker, cotangent, preferred_element_type=jnp.float32)
    cot_rows = (row_weight.reshape(-1, 1) * cot_picked).astype(jnp.bfloat16)
    shape = (experts, 2 * capacity, tokens.shape[1])
    return flat, jnp.stack([token_rows.reshape(shape), cot_rows.reshape(shape)], axis=1)


def scaled(values, scale, first_row):
    rows, hidden = values.shape
    blocks = (first_row + jnp.arange(rows, dtype=jnp.int32)) // BLOCK
    pick = (blocks[:, None] == jnp.arange(scale.shape[0], dtype=jnp.int32)[None, :])[:, :, None]
    of_row = jnp.sum(jnp.where(pick, scale[None], jnp.float32(0.0)), axis=1)
    spread = jnp.repeat(of_row, hidden // scale.shape[1], axis=1)
    return (values.astype(jnp.float32) * spread).astype(jnp.bfloat16)


def on_device(
    tokens,
    cotangent,
    route_weight,
    expert_ids,
    live_tokens,
    replica_plan,
    w_gate,
    w_up,
    w_down,
    scale_gate,
    scale_up,
    scale_down,
):
    members = lax.axis_size("expert")
    slot_count = members // HSH
    width = tokens.shape[1]
    first_row = lax.axis_index("dp") * w_gate.shape[0]
    weights = jnp.stack(
        [
            scaled(w_gate, scale_gate, first_row),
            scaled(w_up, scale_up, first_row),
            scaled(w_down.T, scale_down.T, first_row),
        ]
    )
    flat, rows = route_rows(
        tokens,
        cotangent,
        route_weight,
        expert_ids,
        live_tokens[0],
        replica_plan[0],
        slot_count,
        CAP,
    )
    full, arrived = gather(weights, rows)
    full = full.reshape(3, -1, full.shape[-1])
    mine = lax.dynamic_index_in_dim(
        arrived, lax.axis_index("expert") // HSH, axis=0, keepdims=False
    ).reshape(2, -1, width)
    token_rows, cot_rows = mine[0], mine[1]
    gate_w, up_w, down_w = full[0], full[1], full[2]
    by_rows = (((0,), (0,)), ((), ()))
    by_hidden = (((1,), (1,)), ((), ()))
    f32 = jnp.float32
    bf16 = jnp.bfloat16
    gate_pre = jnp.dot(token_rows, gate_w, preferred_element_type=f32)
    up_pre = jnp.dot(token_rows, up_w, preferred_element_type=f32)
    d_hidden = jnp.dot(cot_rows, down_w, preferred_element_type=f32)
    gate_sig = jax.nn.sigmoid(gate_pre)
    swish = gate_pre * gate_sig
    hidden = (swish * up_pre).astype(bf16)
    d_up = (d_hidden * swish).astype(bf16)
    d_gate = (d_hidden * up_pre * gate_sig * (1.0 + gate_pre * (1.0 - gate_sig))).astype(bf16)
    terms = jnp.stack(
        [
            lax.dot_general(token_rows, d_gate, by_rows, preferred_element_type=f32).astype(bf16),
            lax.dot_general(token_rows, d_up, by_rows, preferred_element_type=f32).astype(bf16),
            lax.dot_general(cot_rows, hidden, by_rows, preferred_element_type=f32).astype(bf16),
        ]
    ).reshape(3, NX * NX, -1, gate_w.shape[1])
    dx = lax.dot_general(d_gate, gate_w, by_hidden, preferred_element_type=f32)
    dx = dx + lax.dot_general(d_up, up_w, by_hidden, preferred_element_type=f32)
    dx = dx.astype(bf16).reshape(NZ, 2, ROWS, width)
    grads, dx_rows = reduce_back(terms, dx)
    d_tokens = jnp.dot(
        flat.astype(bf16), dx_rows.reshape(-1, width), preferred_element_type=f32
    ).astype(bf16)
    return (d_tokens, grads[0], grads[1], grads[2].T)


def solution(mesh):
    return jax.shard_map(
        on_device,
        mesh=mesh,
        in_specs=(
            P(("dp", "expert"), None),
            P(("dp", "expert"), None),
            P(("dp", "expert"), None),
            P(("dp", "expert"), None),
            P(("dp", "expert")),
            P(("dp", "expert"), None),
            P("dp", "expert"),
            P("dp", "expert"),
            P("expert", "dp"),
            P(None, "expert"),
            P(None, "expert"),
            P("expert", None),
        ),
        out_specs=(
            P(("dp", "expert"), None),
            P("dp", "expert"),
            P("dp", "expert"),
            P("expert", "dp"),
        ),
        check_vma=False,
    )
```

```python
import functools

import jax
import jax.numpy as jnp
from jax import lax
from jax.experimental import pallas as pl
from jax.experimental.pallas import tpu as pltpu
from jax.sharding import PartitionSpec as P

HSH = 8
CAP = 4
BLOCK = 128
MESH = pl.DeviceIdType.MESH

NX = 4
NZ = 16
SEG = 4
ROWS = 2 * CAP

HALF = ((0, 112), (112, 112))
PART = (((0, 64), (64, 48)), ((112, 48), (160, 64)))

HOPS = 10


def passes_on(h, r, q):
    d = (h + 3 - q) // 4
    p = (q - h) % 4
    if r == 0:
        return d == 0 and q < 3
    if r == 1:
        return d == 0 or (d == 1 and q < 3)
    return p >= 2 and (d <= 1 or (d == 2 and q < 3))


def onward(h, r):
    return tuple(q for q in range(4) if passes_on(h, r, q))


def arrives(h, r):
    return tuple(q for q in range(4) if h > 0 and passes_on(h - 1, r, (q - 1) % 4))


def kept(h, r):
    return tuple(q for q in arrives(h, r) if (h + 3 - q) // 4 == r)


def lands(h, r):
    return tuple(q for q in onward(h, r) if (q + 1) % 4 in kept(h + 1, r))


def when_in(q, places, body):
    if not places:
        return
    if len(places) == 4:
        body()
        return
    test = q == places[0]
    for place in places[1:]:
        test = test | (q == place)
    pl.when(test)(body)


def place_of():
    g = lax.axis_index("dp")
    j = lax.axis_index("expert")
    return g // NX, g % NX, j // 2, j % 2


def greet(neighbours):
    barrier = pltpu.get_barrier_semaphore()
    for device in neighbours:
        pl.semaphore_signal(barrier, inc=1, device_id=device, device_id_type=MESH)
    pl.semaphore_wait(barrier, len(neighbours))


def at_offset(x, y, axis, offset):
    if axis == 0:
        return ((x + offset) % NX) * NX + y
    return x * NX + (y + offset) % NX


def block_at(x, y, half, i, k):
    if half == 0:
        return ((x + i) % NX) * NX + (y + k) % NX
    return ((x + k) % NX) * NX + (y + i) % NX


def remote(src, dst, send, recv, device):
    return pltpu.make_async_remote_copy(
        src_ref=src,
        dst_ref=dst,
        send_sem=send,
        recv_sem=recv,
        device_id=device,
        device_id_type=MESH,
    )


def gather_kernel(
    w_ref, rows_ref, full_ref, f_ref, u_ref, w_send, w_recv, z_send, z_recv, p_send, p_recv, own_sem
):
    x, y, z, c = place_of()
    g = x * NX + y
    j = z * 2 + c
    seg = z // SEG
    partner = (g, z * 2 + 1 - c)

    def across(axis, way):
        return (at_offset(x, y, axis, way), j)

    def along(way):
        return (g, ((z + way + NZ) % NZ) * 2 + c)

    greet(
        [across(0, 1), across(0, -1), across(1, 1), across(1, -1), along(1), along(-1), partner]
    )

    keep_w = pltpu.make_async_copy(w_ref, full_ref.at[:, g], own_sem.at[0])
    keep_rows = pltpu.make_async_copy(rows_ref.at[seg], f_ref.at[:, z, c], own_sem.at[1])

    def place(way):
        q = z % SEG
        return q if way == 1 else SEG - 1 - q

    def row_block(way, h, r):
        s = (z - way * h + NZ) % NZ
        e = (s // SEG + way * r + SEG) % SEG
        return s, e

    def row_copy(way, h, r, keeps, lands_kept):
        n = 0 if way == 1 else 1
        s, e = row_block(way, h, r)
        if h == 0:
            src = rows_ref.at[e]
        else:
            src = f_ref.at[:, s, c] if keeps else u_ref.at[e, :, s]
        dst = f_ref.at[:, s, c] if lands_kept else u_ref.at[e, :, s]
        return remote(src, dst, z_send.at[n, h, r], z_recv.at[n, h + 1, r], along(way))

    def row_arrival(way, h, r, keeps):
        n = 0 if way == 1 else 1
        s, e = row_block(way, h, r)
        slot = f_ref.at[:, s, c] if keeps else u_ref.at[e, :, s]
        return remote(slot, slot, z_send.at[n, h, r], z_recv.at[n, h, r], along(way))

    def share(way, h):
        n = 0 if way == 1 else 1
        s = (z - way * h + NZ) % NZ
        slot = f_ref.at[:, s, c]
        src = rows_ref.at[seg] if h == 0 else slot
        return remote(src, slot, p_send.at[n, h], p_recv.at[n, h], partner)

    def shared(way, h):
        n = 0 if way == 1 else 1
        s = (z - way * h + NZ) % NZ
        slot = f_ref.at[:, s, 1 - c]
        return remote(slot, slot, p_send.at[n, h], p_recv.at[n, h], partner)

    def row_step(h):
        for r in (2, 1, 0):
            for way in (1, -1):
                q = place(way)
                mine, on, to_kept = kept(h, r), onward(h, r), lands(h, r)
                through = tuple(p for p in arrives(h, r) if p not in mine)

                def arrived(keeps, way=way, r=r):
                    row_arrival(way, h, r, keeps).wait_recv()

                def go(keeps, lands_kept, way=way, r=r):
                    row_copy(way, h, r, keeps, lands_kept).start()

                when_in(q, mine, functools.partial(arrived, True))
                when_in(q, through, functools.partial(arrived, False))
                for keeps in (True, False):
                    for lands_kept in (True, False):
                        places = tuple(
                            p for p in on if (p in mine) == keeps and (p in to_kept) == lands_kept
                        )
                        when_in(q, places, functools.partial(go, keeps, lands_kept))
                when_in(q, mine, lambda way=way: share(way, h).start())

    def w_copy(half, stage, way, part):
        first, second = (0, 1) if half == 0 else (1, 0)
        axis = first if stage == 0 else second
        i = 0 if stage == 0 else (0, 1, -1, 2)[stage - 1]
        if part is None:
            start, size = HALF[half]
            back = 0
        else:
            start, size = PART[half][part]
            back = -way
        if stage == 0:
            owner = block_at(x, y, half, back, 0)
        else:
            owner = block_at(x, y, half, i, back)
        slot = full_ref.at[:, owner, pl.ds(start, size)]
        own = part is None and (stage == 0 or i == 0)
        src = w_ref.at[:, pl.ds(start, size)] if own else slot
        n = 2 * (0 if part is None else 1) + (0 if way == 1 else 1)
        return remote(
            src, slot, w_send.at[half, stage, n], w_recv.at[half, stage, n], across(axis, way)
        )

    def w_arrival(half, stage, way, part):
        first, second = (0, 1) if half == 0 else (1, 0)
        axis = first if stage == 0 else second
        i = 0 if stage == 0 else (0, 1, -1, 2)[stage - 1]
        start, size = HALF[half] if part is None else PART[half][part]
        back = -way if part is None else -2 * way
        owner = block_at(x, y, half, back, 0) if stage == 0 else block_at(x, y, half, i, back)
        slot = full_ref.at[:, owner, pl.ds(start, size)]
        n = 2 * (0 if part is None else 1) + (0 if way == 1 else 1)
        return remote(
            slot, slot, w_send.at[half, stage, n], w_recv.at[half, stage, n], across(axis, way)
        )

    def w_start(stage):
        for half in (0, 1):
            for way in (1, -1):
                w_copy(half, stage, way, None).start()

    def w_forward(stage, then=None):
        for way in (1, -1):
            for half in (0, 1):
                w_arrival(half, stage, way, None).wait_recv()
                w_copy(half, stage, way, 0 if way == 1 else 1).start()
                if then is not None:
                    for other in (1, -1):
                        w_copy(half, then[way], other, None).start()

    row_step(0)
    w_start(0)
    w_start(1)
    share(1, 0).start()
    keep_w.start()
    keep_rows.start()
    row_step(1)
    w_forward(0, {1: 3, -1: 2})
    row_step(2)
    w_forward(1)
    for half in (0, 1):
        for way in (1, -1):
            w_arrival(half, 0, way, 0 if way == 1 else 1).wait_recv()
    w_start(4)
    row_step(3)
    w_forward(3)
    row_step(4)
    w_forward(2)
    row_step(5)
    w_forward(4)
    for h in range(6, HOPS):
        row_step(h)

    for stage in range(5):
        for half in (0, 1):
            for way in (1, -1):
                part = 0 if way == 1 else 1
                if stage > 0:
                    w_arrival(half, stage, way, part).wait_recv()
                w_copy(half, stage, way, None).wait_send()
                w_copy(half, stage, way, part).wait_send()
    share(1, 0).wait_send()
    shared(1, 0).wait_recv()
    for h in range(HOPS):
        for way in (1, -1):
            q = place(way)
            for r in (2, 1, 0):
                when_in(
                    q,
                    onward(h, r),
                    lambda way=way, r=r: row_copy(way, h, r, False, False).wait_send(),
                )

                def end_share(way=way):
                    share(way, h).wait_send()
                    shared(way, h).wait_recv()

                when_in(q, kept(h, r), end_share)
    keep_w.wait()
    keep_rows.wait()


def gather(weights, rows):
    kinds, depth, hidden = weights.shape
    experts, streams, count, width = rows.shape
    dma = pltpu.SemaphoreType.DMA
    return pl.pallas_call(
        gather_kernel,
        out_shape=(
            jax.ShapeDtypeStruct((kinds, NX * NX, depth, hidden), jnp.bfloat16),
            jax.ShapeDtypeStruct((streams, NZ, 2, count, width), jnp.bfloat16),
            jax.ShapeDtypeStruct((experts, streams, NZ, count, width), jnp.bfloat16),
        ),
        in_specs=[pl.BlockSpec(memory_space=pl.ANY)] * 2,
        out_specs=(pl.BlockSpec(memory_space=pl.ANY),) * 3,
        scratch_shapes=[
            dma((2, 5, 4)),
            dma((2, 5, 4)),
            dma((2, HOPS + 1, 3)),
            dma((2, HOPS + 1, 3)),
            dma((2, HOPS)),
            dma((2, HOPS)),
            dma((2,)),
        ],
        compiler_params=pltpu.CompilerParams(collective_id=0, has_side_effects=True),
    )(weights, rows)


REACH = 6
STAGE_OFFSETS = (0, 1, -1, 2)


def reduce_kernel(
    full_in,
    rows_in,
    grad_ref,
    out_ref,
    w,
    xc,
    xct,
    g_ref,
    dx_ref,
    v_part,
    v_whole,
    theirs,
    total,
    held,
    near,
    last,
    v_send,
    v_recv,
    e_send,
    e_recv,
    h_send,
    h_recv,
    l_recv,
    p_sem,
    in_sem,
):
    x, y, z, c = place_of()
    g = x * NX + y
    j = z * 2 + c
    seg = z // SEG
    partner = (g, z * 2 + 1 - c)
    f32 = jnp.float32
    bf16 = jnp.bfloat16
    kinds, depth = grad_ref.shape[:2]
    width = xc.shape[2]

    loads = [
        pltpu.make_async_copy(src, dst, in_sem.at[n])
        for n, (src, dst) in enumerate(
            (
                (rows_in.at[0], xc.at[0]),
                (rows_in.at[1], xc.at[1]),
                (full_in.at[0], w.at[0]),
                (full_in.at[1], w.at[1]),
                (full_in.at[2], w.at[2]),
            )
        )
    ]
    for load in loads:
        load.start()

    def across(axis, way):
        return (at_offset(x, y, axis, way), j)

    def along(offset):
        return (g, ((z + offset + NZ) % NZ) * 2 + c)

    greet(
        [across(0, 1), across(0, -1), across(1, 1), across(1, -1), partner]
        + [along(way * t) for t in range(1, REACH + 1) for way in (1, -1)]
    )

    def owner_of(half, stage, back):
        if stage == 0:
            return block_at(x, y, half, back, 0)
        return block_at(x, y, half, STAGE_OFFSETS[stage - 1], back)

    def axis_of(half, stage):
        first, second = (0, 1) if half == 0 else (1, 0)
        return first if stage == 0 else second

    def g_part(m, half, stage, way):
        k = 0 if way == 1 else 1
        start, size = PART[half][k]
        return remote(
            g_ref.at[m, owner_of(half, stage, 2), pl.ds(start, size)],
            v_part.at[half, stage, k, m, pl.ds(0, size)],
            v_send.at[half, stage, k, m],
            v_recv.at[half, stage, k, m],
            across(axis_of(half, stage), way),
        )

    def g_whole(m, half, stage, way):
        k = 0 if way == 1 else 1
        start, size = HALF[half]
        return remote(
            g_ref.at[m, owner_of(half, stage, way), pl.ds(start, size)],
            v_whole.at[half, stage, k, m],
            v_send.at[half, stage, 2 + k, m],
            v_recv.at[half, stage, 2 + k, m],
            across(axis_of(half, stage), way),
        )

    def parts_in(stage):
        def one(m, _):
            for half in (0, 1):
                for way in (1, -1):
                    k = 0 if way == 1 else 1
                    start, size = PART[half][k]
                    g_part(m, half, stage, way).wait_recv()
                    block = owner_of(half, stage, way)
                    here = g_ref[m, block, pl.ds(start, size), :].astype(f32)
                    came = v_part[half, stage, k, m, pl.ds(0, size), :].astype(f32)
                    g_ref[m, block, pl.ds(start, size), :] = (here + came).astype(bf16)
                    g_whole(m, half, stage, way).start()
            return 0

        lax.fori_loop(0, kinds, one, 0)

    def wholes_in(stage, then=False):
        def one(m, _):
            for half in (0, 1):
                start, size = HALF[half]
                g_whole(m, half, stage, 1).wait_recv()
                g_whole(m, half, stage, -1).wait_recv()
                block = owner_of(half, stage, 0)
                here = g_ref[m, block, pl.ds(start, size), :].astype(f32)
                left = v_whole[half, stage, 0, m].astype(f32)
                right = v_whole[half, stage, 1, m].astype(f32)
                summed = (here + left + right).astype(bf16)
                if stage == 0:
                    grad_ref[m, pl.ds(start, size), :] = summed
                else:
                    g_ref[m, block, pl.ds(start, size), :] = summed
                if then:
                    for way in (1, -1):
                        g_part(m, half, 0, way).start()
            return 0

        lax.fori_loop(0, kinds, one, 0)

    def place(way):
        q = z % SEG
        return q if way == 1 else SEG - 1 - q

    def slots(way, kind, n):
        side = 0 if way == 1 else 1
        if kind == "near":
            return near.at[side, n], h_recv.at[side, n]
        if kind == "held":
            return held.at[side, n], e_recv.at[side, n]
        return last.at[side, n], l_recv.at[side, n]

    def item_sem(way, kind, n):
        side = 0 if way == 1 else 1
        return h_send.at[side, n] if kind == "near" else e_send.at[side, n]

    def await_item(way, kind, n):
        slot, recv = slots(way, kind, n)
        remote(slot, slot, recv, recv, along(way)).wait_recv()

    def send_item(way, kind, n, q):
        s = (z - way * (n if kind == "near" else q + n) + 2 * NZ) % NZ
        src = total.at[s] if q == SEG - 1 else slots(way, kind, n)[0]
        if kind == "near":
            dst, recv = slots(way, "near", n - 1) if n > 1 else slots(way, "last", 0)
            target = along(-way)
        elif q > 0:
            dst, recv = slots(way, "held", n)
            target = along(-way)
        else:
            dst, recv = slots(way, "last", 1 if n <= SEG else 2)
            target = along(-way * n)
        return remote(src, dst, item_sem(way, kind, n), recv, target)

    def items_of(q):
        return [("held", t) for t in range(REACH, 0, -1)] + [("near", h) for h in range(q, 0, -1)]

    def item_step(way, kind, n, q):
        if q < SEG - 1:
            side = 0 if way == 1 else 1
            s = (z - way * (n if kind == "near" else q + n) + 2 * NZ) % NZ
            await_item(way, kind, n)
            slot = near if kind == "near" else held
            slot[side, n] = (slot[side, n].astype(f32) + total[s].astype(f32)).astype(bf16)
        send_item(way, kind, n, q).start()

    def back_round(depth_from_far):
        for way in (1, -1):
            q = SEG - 1 - depth_from_far

            def go(way=way, q=q):
                for kind, n in items_of(q):
                    item_step(way, kind, n, q)

            pl.when(place(way) == q)(go)

    loads[0].wait()
    loads[1].wait()

    def turn(n, _):
        at = pl.ds(pl.multiple_of(n * 256, 256), 256)
        xct[0, at, :] = xc[0, :, at].T
        xct[1, at, :] = xc[1, :, at].T
        return 0

    lax.fori_loop(0, width // 256, turn, 0)
    loads[2].wait()
    gate_pre = jnp.dot(xc[0], w[0], preferred_element_type=f32)
    loads[3].wait()
    up_pre = jnp.dot(xc[0], w[1], preferred_element_type=f32)
    loads[4].wait()
    d_hidden = jnp.dot(xc[1], w[2], preferred_element_type=f32)
    gate_sig = jax.nn.sigmoid(gate_pre)
    swish = gate_pre * gate_sig
    hidden = (swish * up_pre).astype(bf16)
    d_up = (d_hidden * swish).astype(bf16)
    d_gate = (d_hidden * up_pre * gate_sig * (1.0 + gate_pre * (1.0 - gate_sig))).astype(bf16)

    def block_terms(i, k):
        block = block_at(x, y, 0, i, k)
        at = pl.ds(pl.multiple_of(block * depth, 16), depth)
        for m, (stream, right) in enumerate(((0, d_gate), (0, d_up), (1, hidden))):
            g_ref[m, block] = jnp.dot(xct[stream, at, :], right, preferred_element_type=f32).astype(
                bf16
            )
            if k == 2:
                stage = 1 + STAGE_OFFSETS.index(i)
                g_part(m, 0, stage, 1).start()
                g_part(m, 0, stage, -1).start()
            if i == 2:
                stage = 1 + STAGE_OFFSETS.index(k)
                g_part(m, 1, stage, 1).start()
                g_part(m, 1, stage, -1).start()

    first_blocks = ((2, 2), (1, 2), (2, 1), (-1, 2), (2, -1), (0, 2), (2, 0))
    for i, k in first_blocks:
        block_terms(i, k)

    by_hidden = (((1,), (1,)), ((), ()))
    chunk = 512

    def dx_chunk(n, _):
        at = pl.ds(pl.multiple_of(n * chunk, chunk), chunk)
        part = lax.dot_general(d_gate, w[0, at, :], by_hidden, preferred_element_type=f32)
        part = part + lax.dot_general(d_up, w[1, at, :], by_hidden, preferred_element_type=f32)
        dx_ref[:, :, :, at] = part.reshape(NZ, 2, ROWS, chunk).astype(bf16)
        return 0

    lax.fori_loop(0, width // chunk, dx_chunk, 0)
    swap = remote(dx_ref.at[:, 1 - c], theirs, p_sem.at[0], p_sem.at[1], partner)
    swap.start()
    for i in (1, -1, 0):
        for k in (1, -1, 0):
            block_terms(i, k)

    parts_in(4)
    swap.wait()

    def own_total(s, _):
        total[s] = (dx_ref[s, c].astype(f32) + theirs[s].astype(f32)).astype(bf16)
        return 0

    lax.fori_loop(0, NZ, own_total, 0)
    back_round(0)
    parts_in(2)
    back_round(1)
    parts_in(3)
    wholes_in(4, True)
    back_round(2)
    parts_in(1)
    back_round(3)
    wholes_in(2)
    wholes_in(3)
    parts_in(0)

    out_ref[seg] = total[z]

    def take(way, n):
        side = 0 if way == 1 else 1
        await_item(way, "last", n)
        if n == 0:
            out_ref[seg] = (out_ref[seg].astype(f32) + last[side, 0].astype(f32)).astype(bf16)
        else:
            out_ref[(seg + way * n + SEG) % SEG] = last[side, n]

    for way in (1, -1):
        when_in(place(way), (0, 1, 2), functools.partial(take, way, 0))
        take(way, 1)
        when_in(place(way), (2, 3), functools.partial(take, way, 2))

    wholes_in(1)
    wholes_in(0)

    def sent(m, _):
        for stage in range(5):
            for half in (0, 1):
                for way in (1, -1):
                    g_part(m, half, stage, way).wait_send()
                    g_whole(m, half, stage, way).wait_send()
        return 0

    lax.fori_loop(0, kinds, sent, 0)
    for way in (1, -1):
        for q in range(SEG):

            def ended(way=way, q=q):
                for kind, n in items_of(q):
                    send_item(way, kind, n, q).wait_send()

            pl.when(place(way) == q)(ended)


def layer_and_reduce(full, rows):
    kinds, whole_depth, hidden = full.shape
    streams, count, width = rows.shape
    groups = NX * NX
    depth = whole_depth // groups
    dma = pltpu.SemaphoreType.DMA
    vmem = pltpu.VMEM
    bf16 = jnp.bfloat16
    return pl.pallas_call(
        reduce_kernel,
        out_shape=(
            jax.ShapeDtypeStruct((kinds, depth, hidden), bf16),
            jax.ShapeDtypeStruct((SEG, ROWS, width), bf16),
        ),
        in_specs=[pl.BlockSpec(memory_space=pl.ANY)] * 2,
        out_specs=(pl.BlockSpec(memory_space=pltpu.VMEM),) * 2,
        scratch_shapes=[
            vmem((kinds, whole_depth, hidden), bf16),
            vmem((streams, count, width), bf16),
            vmem((streams, width, count), bf16),
            vmem((kinds, groups, depth, hidden), bf16),
            vmem((NZ, 2, ROWS, width), bf16),
            vmem((2, 5, 2, kinds, 64, hidden), bf16),
            vmem((2, 5, 2, kinds, 112, hidden), bf16),
            vmem((NZ, ROWS, width), bf16),
            vmem((NZ, ROWS, width), bf16),
            vmem((2, REACH + 1, ROWS, width), bf16),
            vmem((2, SEG, ROWS, width), bf16),
            vmem((2, 3, ROWS, width), bf16),
            dma((2, 5, 4, 3)),
            dma((2, 5, 4, 3)),
            dma((2, REACH + 1)),
            dma((2, REACH + 1)),
            dma((2, SEG)),
            dma((2, SEG)),
            dma((2, 3)),
            dma((2,)),
            dma((5,)),
        ],
        compiler_params=pltpu.CompilerParams(collective_id=1, has_side_effects=True),
    )(full, rows)


def route_rows(tokens, cotangent, route_weight, expert_ids, live_count, plan, experts, capacity):
    count = tokens.shape[0]
    token_index = jnp.arange(count, dtype=jnp.int32)
    expert_index = jnp.arange(experts, dtype=jnp.int32)
    matches = expert_ids[:, None, :] == expert_index[None, :, None]
    routed = jnp.any(matches, axis=2) & (token_index < live_count)[:, None]
    to_replica = (token_index % 2 == 1)[:, None] & (plan[None, :] == 1)
    in_lists = jnp.stack([routed & ~to_replica, routed & to_replica], axis=2).astype(jnp.int32)
    position = jnp.cumsum(in_lists, axis=0) - 1
    capacity_index = jnp.arange(capacity, dtype=jnp.int32)
    selected = ((in_lists[..., None] == 1) & (position[..., None] == capacity_index)).astype(
        jnp.float32
    )
    weight_sum = jnp.sum(jnp.where(matches, route_weight[:, None, :], jnp.float32(0.0)), axis=2)
    row_weight = jnp.sum(selected * weight_sum[:, :, None, None], axis=0)
    flat = selected.reshape(count, -1)
    picker = flat.T.astype(jnp.bfloat16)
    token_rows = jnp.dot(picker, tokens, preferred_element_type=jnp.float32).astype(jnp.bfloat16)
    cot_picked = jnp.dot(picker, cotangent, preferred_element_type=jnp.float32)
    cot_rows = (row_weight.reshape(-1, 1) * cot_picked).astype(jnp.bfloat16)
    shape = (experts, 2 * capacity, tokens.shape[1])
    return flat, jnp.stack([token_rows.reshape(shape), cot_rows.reshape(shape)], axis=1)


def scaled(values, scale, first_row):
    rows, hidden = values.shape
    blocks = (first_row + jnp.arange(rows, dtype=jnp.int32)) // BLOCK
    pick = (blocks[:, None] == jnp.arange(scale.shape[0], dtype=jnp.int32)[None, :])[:, :, None]
    of_row = jnp.sum(jnp.where(pick, scale[None], jnp.float32(0.0)), axis=1)
    spread = jnp.repeat(of_row, hidden // scale.shape[1], axis=1)
    return (values.astype(jnp.float32) * spread).astype(jnp.bfloat16)


def on_device(
    tokens,
    cotangent,
    route_weight,
    expert_ids,
    live_tokens,
    replica_plan,
    w_gate,
    w_up,
    w_down,
    scale_gate,
    scale_up,
    scale_down,
):
    members = lax.axis_size("expert")
    slot_count = members // HSH
    width = tokens.shape[1]
    first_row = lax.axis_index("dp") * w_gate.shape[0]
    weights = jnp.stack(
        [
            scaled(w_gate, scale_gate, first_row),
            scaled(w_up, scale_up, first_row),
            scaled(w_down.T, scale_down.T, first_row),
        ]
    )
    flat, rows = route_rows(
        tokens,
        cotangent,
        route_weight,
        expert_ids,
        live_tokens[0],
        replica_plan[0],
        slot_count,
        CAP,
    )
    full, arrived, _ = gather(weights, rows)
    grads, dx_rows = layer_and_reduce(
        full.reshape(full.shape[0], -1, full.shape[-1]), arrived.reshape(2, -1, width)
    )
    bf16, f32 = jnp.bfloat16, jnp.float32
    d_tokens = jnp.dot(
        flat.astype(bf16), dx_rows.reshape(-1, width), preferred_element_type=f32
    ).astype(bf16)
    return (d_tokens, grads[0], grads[1], grads[2].T)


def solution(mesh):
    return jax.shard_map(
        on_device,
        mesh=mesh,
        in_specs=(
            P(("dp", "expert"), None),
            P(("dp", "expert"), None),
            P(("dp", "expert"), None),
            P(("dp", "expert"), None),
            P(("dp", "expert")),
            P(("dp", "expert"), None),
            P("dp", "expert"),
            P("dp", "expert"),
            P("expert", "dp"),
            P(None, "expert"),
            P(None, "expert"),
            P("expert", None),
        ),
        out_specs=(
            P(("dp", "expert"), None),
            P("dp", "expert"),
            P("dp", "expert"),
            P("expert", "dp"),
        ),
        check_vma=False,
    )
```

```python
import functools

import jax
import jax.numpy as jnp
from jax import lax
from jax.experimental import pallas as pl
from jax.experimental.pallas import tpu as pltpu
from jax.sharding import PartitionSpec as P

HSH = 8
CAP = 4
BLOCK = 128
MESH = pl.DeviceIdType.MESH

NX = 4
NZ = 16
SEG = 4
ROWS = 2 * CAP

HALF = ((0, 112), (112, 112))
PART = (((0, 64), (64, 48)), ((112, 48), (160, 64)))

HOPS = 10


def passes_on(h, r, q):
    d = (h + 3 - q) // 4
    p = (q - h) % 4
    if r == 0:
        return d == 0 and q < 3
    if r == 1:
        return d == 0 or (d == 1 and q < 3)
    return p >= 2 and (d <= 1 or (d == 2 and q < 3))


def onward(h, r):
    return tuple(q for q in range(4) if passes_on(h, r, q))


def arrives(h, r):
    return tuple(q for q in range(4) if h > 0 and passes_on(h - 1, r, (q - 1) % 4))


def kept(h, r):
    return tuple(q for q in arrives(h, r) if (h + 3 - q) // 4 == r)


def lands(h, r):
    return tuple(q for q in onward(h, r) if (q + 1) % 4 in kept(h + 1, r))


def when_in(q, places, body):
    if not places:
        return
    if len(places) == 4:
        body()
        return
    test = q == places[0]
    for place in places[1:]:
        test = test | (q == place)
    pl.when(test)(body)


def place_of():
    g = lax.axis_index("dp")
    j = lax.axis_index("expert")
    return g // NX, g % NX, j // 2, j % 2


def greet(neighbours):
    barrier = pltpu.get_barrier_semaphore()
    for device in neighbours:
        pl.semaphore_signal(barrier, inc=1, device_id=device, device_id_type=MESH)
    pl.semaphore_wait(barrier, len(neighbours))


def at_offset(x, y, axis, offset):
    if axis == 0:
        return ((x + offset) % NX) * NX + y
    return x * NX + (y + offset) % NX


def block_at(x, y, half, i, k):
    if half == 0:
        return ((x + i) % NX) * NX + (y + k) % NX
    return ((x + k) % NX) * NX + (y + i) % NX


def remote(src, dst, send, recv, device):
    return pltpu.make_async_remote_copy(
        src_ref=src,
        dst_ref=dst,
        send_sem=send,
        recv_sem=recv,
        device_id=device,
        device_id_type=MESH,
    )


def gather_kernel(
    w_ref, rows_ref, full_ref, f_ref, u_ref, w_send, w_recv, z_send, z_recv, p_send, p_recv, own_sem
):
    x, y, z, c = place_of()
    g = x * NX + y
    j = z * 2 + c
    seg = z // SEG
    partner = (g, z * 2 + 1 - c)

    def across(axis, way):
        return (at_offset(x, y, axis, way), j)

    def along(way):
        return (g, ((z + way + NZ) % NZ) * 2 + c)

    greet(
        [across(0, 1), across(0, -1), across(1, 1), across(1, -1), along(1), along(-1), partner]
    )

    keep_w = pltpu.make_async_copy(w_ref, full_ref.at[:, g], own_sem.at[0])
    keep_rows = pltpu.make_async_copy(rows_ref.at[seg], f_ref.at[:, z, c], own_sem.at[1])

    def place(way):
        q = z % SEG
        return q if way == 1 else SEG - 1 - q

    def row_block(way, h, r):
        s = (z - way * h + NZ) % NZ
        e = (s // SEG + way * r + SEG) % SEG
        return s, e

    def row_copy(way, h, r, keeps, lands_kept):
        n = 0 if way == 1 else 1
        s, e = row_block(way, h, r)
        if h == 0:
            src = rows_ref.at[e]
        else:
            src = f_ref.at[:, s, c] if keeps else u_ref.at[e, :, s]
        dst = f_ref.at[:, s, c] if lands_kept else u_ref.at[e, :, s]
        return remote(src, dst, z_send.at[n, h, r], z_recv.at[n, h + 1, r], along(way))

    def row_arrival(way, h, r, keeps):
        n = 0 if way == 1 else 1
        s, e = row_block(way, h, r)
        slot = f_ref.at[:, s, c] if keeps else u_ref.at[e, :, s]
        return remote(slot, slot, z_send.at[n, h, r], z_recv.at[n, h, r], along(way))

    def share(way, h):
        n = 0 if way == 1 else 1
        s = (z - way * h + NZ) % NZ
        slot = f_ref.at[:, s, c]
        src = rows_ref.at[seg] if h == 0 else slot
        return remote(src, slot, p_send.at[n, h], p_recv.at[n, h], partner)

    def shared(way, h):
        n = 0 if way == 1 else 1
        s = (z - way * h + NZ) % NZ
        slot = f_ref.at[:, s, 1 - c]
        return remote(slot, slot, p_send.at[n, h], p_recv.at[n, h], partner)

    def row_step(h):
        for r in (2, 1, 0):
            for way in (1, -1):
                q = place(way)
                mine, on, to_kept = kept(h, r), onward(h, r), lands(h, r)
                through = tuple(p for p in arrives(h, r) if p not in mine)

                def arrived(keeps, way=way, r=r):
                    row_arrival(way, h, r, keeps).wait_recv()

                def go(keeps, lands_kept, way=way, r=r):
                    row_copy(way, h, r, keeps, lands_kept).start()

                when_in(q, mine, functools.partial(arrived, True))
                when_in(q, through, functools.partial(arrived, False))
                for keeps in (True, False):
                    for lands_kept in (True, False):
                        places = tuple(
                            p for p in on if (p in mine) == keeps and (p in to_kept) == lands_kept
                        )
                        when_in(q, places, functools.partial(go, keeps, lands_kept))
                when_in(q, mine, lambda way=way: share(way, h).start())

    def w_copy(half, stage, way, part):
        first, second = (0, 1) if half == 0 else (1, 0)
        axis = first if stage == 0 else second
        i = 0 if stage == 0 else (0, 1, -1, 2)[stage - 1]
        if part is None:
            start, size = HALF[half]
            back = 0
        else:
            start, size = PART[half][part]
            back = -way
        if stage == 0:
            owner = block_at(x, y, half, back, 0)
        else:
            owner = block_at(x, y, half, i, back)
        slot = full_ref.at[:, owner, pl.ds(start, size)]
        own = part is None and (stage == 0 or i == 0)
        src = w_ref.at[:, pl.ds(start, size)] if own else slot
        n = 2 * (0 if part is None else 1) + (0 if way == 1 else 1)
        return remote(
            src, slot, w_send.at[half, stage, n], w_recv.at[half, stage, n], across(axis, way)
        )

    def w_arrival(half, stage, way, part):
        first, second = (0, 1) if half == 0 else (1, 0)
        axis = first if stage == 0 else second
        i = 0 if stage == 0 else (0, 1, -1, 2)[stage - 1]
        start, size = HALF[half] if part is None else PART[half][part]
        back = -way if part is None else -2 * way
        owner = block_at(x, y, half, back, 0) if stage == 0 else block_at(x, y, half, i, back)
        slot = full_ref.at[:, owner, pl.ds(start, size)]
        n = 2 * (0 if part is None else 1) + (0 if way == 1 else 1)
        return remote(
            slot, slot, w_send.at[half, stage, n], w_recv.at[half, stage, n], across(axis, way)
        )

    def w_start(stage):
        for half in (0, 1):
            for way in (1, -1):
                w_copy(half, stage, way, None).start()

    def w_forward(stage, then=None):
        for way in (1, -1):
            for half in (0, 1):
                w_arrival(half, stage, way, None).wait_recv()
                w_copy(half, stage, way, 0 if way == 1 else 1).start()
                if then is not None:
                    for other in (1, -1):
                        w_copy(half, then[way], other, None).start()

    row_step(0)
    w_start(0)
    w_start(1)
    share(1, 0).start()
    keep_w.start()
    keep_rows.start()
    row_step(1)
    w_forward(0, {1: 3, -1: 2})
    row_step(2)
    w_forward(1)
    for half in (0, 1):
        for way in (1, -1):
            w_arrival(half, 0, way, 0 if way == 1 else 1).wait_recv()
    w_start(4)
    row_step(3)
    w_forward(3)
    row_step(4)
    w_forward(2)
    row_step(5)
    w_forward(4)
    for h in range(6, HOPS):
        row_step(h)

    for stage in range(5):
        for half in (0, 1):
            for way in (1, -1):
                part = 0 if way == 1 else 1
                if stage > 0:
                    w_arrival(half, stage, way, part).wait_recv()
                w_copy(half, stage, way, None).wait_send()
                w_copy(half, stage, way, part).wait_send()
    share(1, 0).wait_send()
    shared(1, 0).wait_recv()
    for h in range(HOPS):
        for way in (1, -1):
            q = place(way)
            for r in (2, 1, 0):
                when_in(
                    q,
                    onward(h, r),
                    lambda way=way, r=r: row_copy(way, h, r, False, False).wait_send(),
                )

                def end_share(way=way):
                    share(way, h).wait_send()
                    shared(way, h).wait_recv()

                when_in(q, kept(h, r), end_share)
    keep_w.wait()
    keep_rows.wait()


def gather(weights, rows):
    kinds, depth, hidden = weights.shape
    experts, streams, count, width = rows.shape
    dma = pltpu.SemaphoreType.DMA
    return pl.pallas_call(
        gather_kernel,
        out_shape=(
            jax.ShapeDtypeStruct((kinds, NX * NX, depth, hidden), jnp.bfloat16),
            jax.ShapeDtypeStruct((streams, NZ, 2, count, width), jnp.bfloat16),
            jax.ShapeDtypeStruct((experts, streams, NZ, count, width), jnp.bfloat16),
        ),
        in_specs=[pl.BlockSpec(memory_space=pl.ANY)] * 2,
        out_specs=(pl.BlockSpec(memory_space=pl.ANY),) * 3,
        scratch_shapes=[
            dma((2, 5, 4)),
            dma((2, 5, 4)),
            dma((2, HOPS + 1, 3)),
            dma((2, HOPS + 1, 3)),
            dma((2, HOPS)),
            dma((2, HOPS)),
            dma((2,)),
        ],
        compiler_params=pltpu.CompilerParams(collective_id=0, has_side_effects=True),
    )(weights, rows)


REACH = 6
STAGE_OFFSETS = (0, 1, -1, 2)


def reduce_kernel(
    full_in,
    rows_in,
    pick_ref,
    d_tokens_ref,
    grad_gate_ref,
    grad_up_ref,
    grad_down_ref,
    out_ref,
    grad_ref,
    w,
    xc,
    xct,
    g_ref,
    dx_ref,
    v_part,
    v_whole,
    theirs,
    total,
    held,
    near,
    last,
    v_send,
    v_recv,
    e_send,
    e_recv,
    h_send,
    h_recv,
    l_recv,
    p_sem,
    in_sem,
):
    x, y, z, c = place_of()
    g = x * NX + y
    j = z * 2 + c
    seg = z // SEG
    partner = (g, z * 2 + 1 - c)
    f32 = jnp.float32
    bf16 = jnp.bfloat16
    kinds, depth = grad_ref.shape[:2]
    width = xc.shape[2]

    loads = [
        pltpu.make_async_copy(src, dst, in_sem.at[n])
        for n, (src, dst) in enumerate(
            (
                (rows_in.at[0], xc.at[0]),
                (rows_in.at[1], xc.at[1]),
                (full_in.at[0], w.at[0]),
                (full_in.at[1], w.at[1]),
                (full_in.at[2], w.at[2]),
            )
        )
    ]
    for load in loads:
        load.start()

    def across(axis, way):
        return (at_offset(x, y, axis, way), j)

    def along(offset):
        return (g, ((z + offset + NZ) % NZ) * 2 + c)

    greet(
        [across(0, 1), across(0, -1), across(1, 1), across(1, -1), partner]
        + [along(way * t) for t in range(1, REACH + 1) for way in (1, -1)]
    )

    def owner_of(half, stage, back):
        if stage == 0:
            return block_at(x, y, half, back, 0)
        return block_at(x, y, half, STAGE_OFFSETS[stage - 1], back)

    def axis_of(half, stage):
        first, second = (0, 1) if half == 0 else (1, 0)
        return first if stage == 0 else second

    def g_part(m, half, stage, way):
        k = 0 if way == 1 else 1
        start, size = PART[half][k]
        return remote(
            g_ref.at[m, owner_of(half, stage, 2), pl.ds(start, size)],
            v_part.at[half, stage, k, m, pl.ds(0, size)],
            v_send.at[half, stage, k, m],
            v_recv.at[half, stage, k, m],
            across(axis_of(half, stage), way),
        )

    def g_whole(m, half, stage, way):
        k = 0 if way == 1 else 1
        start, size = HALF[half]
        return remote(
            g_ref.at[m, owner_of(half, stage, way), pl.ds(start, size)],
            v_whole.at[half, stage, k, m],
            v_send.at[half, stage, 2 + k, m],
            v_recv.at[half, stage, 2 + k, m],
            across(axis_of(half, stage), way),
        )

    def parts_in(stage):
        def one(m, _):
            for half in (0, 1):
                for way in (1, -1):
                    k = 0 if way == 1 else 1
                    start, size = PART[half][k]
                    g_part(m, half, stage, way).wait_recv()
                    block = owner_of(half, stage, way)
                    here = g_ref[m, block, pl.ds(start, size), :].astype(f32)
                    came = v_part[half, stage, k, m, pl.ds(0, size), :].astype(f32)
                    g_ref[m, block, pl.ds(start, size), :] = (here + came).astype(bf16)
                    g_whole(m, half, stage, way).start()
            return 0

        lax.fori_loop(0, kinds, one, 0)

    def wholes_in(stage, then=False):
        def one(m, _):
            for half in (0, 1):
                start, size = HALF[half]
                g_whole(m, half, stage, 1).wait_recv()
                g_whole(m, half, stage, -1).wait_recv()
                block = owner_of(half, stage, 0)
                here = g_ref[m, block, pl.ds(start, size), :].astype(f32)
                left = v_whole[half, stage, 0, m].astype(f32)
                right = v_whole[half, stage, 1, m].astype(f32)
                summed = (here + left + right).astype(bf16)
                if stage == 0:
                    grad_ref[m, pl.ds(start, size), :] = summed
                else:
                    g_ref[m, block, pl.ds(start, size), :] = summed
                if then:
                    for way in (1, -1):
                        g_part(m, half, 0, way).start()
            return 0

        lax.fori_loop(0, kinds, one, 0)

    def place(way):
        q = z % SEG
        return q if way == 1 else SEG - 1 - q

    def slots(way, kind, n):
        side = 0 if way == 1 else 1
        if kind == "near":
            return near.at[side, n], h_recv.at[side, n]
        if kind == "held":
            return held.at[side, n], e_recv.at[side, n]
        return last.at[side, n], l_recv.at[side, n]

    def item_sem(way, kind, n):
        side = 0 if way == 1 else 1
        return h_send.at[side, n] if kind == "near" else e_send.at[side, n]

    def await_item(way, kind, n):
        slot, recv = slots(way, kind, n)
        remote(slot, slot, recv, recv, along(way)).wait_recv()

    def send_item(way, kind, n, q):
        s = (z - way * (n if kind == "near" else q + n) + 2 * NZ) % NZ
        src = total.at[s] if q == SEG - 1 else slots(way, kind, n)[0]
        if kind == "near":
            dst, recv = slots(way, "near", n - 1) if n > 1 else slots(way, "last", 0)
            target = along(-way)
        elif q > 0:
            dst, recv = slots(way, "held", n)
            target = along(-way)
        else:
            dst, recv = slots(way, "last", 1 if n <= SEG else 2)
            target = along(-way * n)
        return remote(src, dst, item_sem(way, kind, n), recv, target)

    def items_of(q):
        return [("held", t) for t in range(REACH, 0, -1)] + [("near", h) for h in range(q, 0, -1)]

    def item_step(way, kind, n, q):
        if q < SEG - 1:
            side = 0 if way == 1 else 1
            s = (z - way * (n if kind == "near" else q + n) + 2 * NZ) % NZ
            await_item(way, kind, n)
            slot = near if kind == "near" else held
            slot[side, n] = (slot[side, n].astype(f32) + total[s].astype(f32)).astype(bf16)
        send_item(way, kind, n, q).start()

    def back_round(depth_from_far):
        for way in (1, -1):
            q = SEG - 1 - depth_from_far

            def go(way=way, q=q):
                for kind, n in items_of(q):
                    item_step(way, kind, n, q)

            pl.when(place(way) == q)(go)

    loads[0].wait()
    loads[1].wait()

    def turn(n, _):
        at = pl.ds(pl.multiple_of(n * 256, 256), 256)
        xct[0, at, :] = xc[0, :, at].T
        xct[1, at, :] = xc[1, :, at].T
        return 0

    lax.fori_loop(0, width // 256, turn, 0)
    loads[2].wait()
    gate_pre = jnp.dot(xc[0], w[0], preferred_element_type=f32)
    loads[3].wait()
    up_pre = jnp.dot(xc[0], w[1], preferred_element_type=f32)
    loads[4].wait()
    d_hidden = jnp.dot(xc[1], w[2], preferred_element_type=f32)
    gate_sig = jax.nn.sigmoid(gate_pre)
    swish = gate_pre * gate_sig
    hidden = (swish * up_pre).astype(bf16)
    d_up = (d_hidden * swish).astype(bf16)
    d_gate = (d_hidden * up_pre * gate_sig * (1.0 + gate_pre * (1.0 - gate_sig))).astype(bf16)

    def block_terms(i, k):
        block = block_at(x, y, 0, i, k)
        at = pl.ds(pl.multiple_of(block * depth, 16), depth)
        for m, (stream, right) in enumerate(((0, d_gate), (0, d_up), (1, hidden))):
            g_ref[m, block] = jnp.dot(xct[stream, at, :], right, preferred_element_type=f32).astype(
                bf16
            )
            if k == 2:
                stage = 1 + STAGE_OFFSETS.index(i)
                g_part(m, 0, stage, 1).start()
                g_part(m, 0, stage, -1).start()
            if i == 2:
                stage = 1 + STAGE_OFFSETS.index(k)
                g_part(m, 1, stage, 1).start()
                g_part(m, 1, stage, -1).start()

    first_blocks = ((2, 2), (1, 2), (2, 1), (-1, 2), (2, -1), (0, 2), (2, 0))
    by_hidden = (((1,), (1,)), ((), ()))
    chunk = 512

    def dx_chunk(n, _):
        at = pl.ds(pl.multiple_of(n * chunk, chunk), chunk)
        part = lax.dot_general(d_gate, w[0, at, :], by_hidden, preferred_element_type=f32)
        part = part + lax.dot_general(d_up, w[1, at, :], by_hidden, preferred_element_type=f32)
        dx_ref[:, :, :, at] = part.reshape(NZ, 2, ROWS, chunk).astype(bf16)
        return 0

    lax.fori_loop(0, width // chunk, dx_chunk, 0)
    swap = remote(dx_ref.at[:, 1 - c], theirs, p_sem.at[0], p_sem.at[1], partner)
    swap.start()
    for i, k in first_blocks:
        block_terms(i, k)
    swap.wait()

    def own_total(s, _):
        total[s] = (dx_ref[s, c].astype(f32) + theirs[s].astype(f32)).astype(bf16)
        return 0

    lax.fori_loop(0, NZ, own_total, 0)
    back_round(0)
    for i in (1, -1, 0):
        for k in (1, -1, 0):
            block_terms(i, k)

    parts_in(4)
    parts_in(2)
    parts_in(3)
    back_round(1)
    wholes_in(4, True)
    parts_in(1)
    back_round(2)
    wholes_in(2)
    back_round(3)
    wholes_in(3)
    parts_in(0)

    out_ref[seg] = total[z]

    def take(way, n):
        side = 0 if way == 1 else 1
        await_item(way, "last", n)
        if n == 0:
            out_ref[seg] = (out_ref[seg].astype(f32) + last[side, 0].astype(f32)).astype(bf16)
        else:
            out_ref[(seg + way * n + SEG) % SEG] = last[side, n]

    for way in (1, -1):
        when_in(place(way), (0, 1, 2), functools.partial(take, way, 0))
        take(way, 1)
        when_in(place(way), (2, 3), functools.partial(take, way, 2))

    wholes_in(1)
    d_tokens_ref[...] = lax.dot_general(
        pick_ref[...],
        out_ref[...].astype(f32).reshape(SEG * ROWS, width).astype(bf16),
        (((0,), (0,)), ((), ())),
        preferred_element_type=f32,
    ).astype(bf16)
    wholes_in(0)
    grad_gate_ref[...] = grad_ref[0]
    grad_up_ref[...] = grad_ref[1]
    grad_down_ref[...] = grad_ref[2]

    def sent(m, _):
        for stage in range(5):
            for half in (0, 1):
                for way in (1, -1):
                    g_part(m, half, stage, way).wait_send()
                    g_whole(m, half, stage, way).wait_send()
        return 0

    lax.fori_loop(0, kinds, sent, 0)
    for way in (1, -1):
        for q in range(SEG):

            def ended(way=way, q=q):
                for kind, n in items_of(q):
                    send_item(way, kind, n, q).wait_send()

            pl.when(place(way) == q)(ended)


def layer_and_reduce(full, rows, picker):
    kinds, whole_depth, hidden = full.shape
    streams, count, width = rows.shape
    groups = NX * NX
    depth = whole_depth // groups
    dma = pltpu.SemaphoreType.DMA
    vmem = pltpu.VMEM
    bf16 = jnp.bfloat16
    return pl.pallas_call(
        reduce_kernel,
        out_shape=(
            jax.ShapeDtypeStruct((picker.shape[1], width), bf16),
            jax.ShapeDtypeStruct((depth, hidden), bf16),
            jax.ShapeDtypeStruct((depth, hidden), bf16),
            jax.ShapeDtypeStruct((depth, hidden), bf16),
        ),
        in_specs=[pl.BlockSpec(memory_space=pl.ANY)] * 2
        + [pl.BlockSpec(memory_space=pltpu.VMEM)],
        out_specs=(pl.BlockSpec(memory_space=pltpu.VMEM),) * 4,
        scratch_shapes=[
            vmem((SEG, ROWS, width), bf16),
            vmem((kinds, depth, hidden), bf16),
            vmem((kinds, whole_depth, hidden), bf16),
            vmem((streams, count, width), bf16),
            vmem((streams, width, count), bf16),
            vmem((kinds, groups, depth, hidden), bf16),
            vmem((NZ, 2, ROWS, width), bf16),
            vmem((2, 5, 2, kinds, 64, hidden), bf16),
            vmem((2, 5, 2, kinds, 112, hidden), bf16),
            vmem((NZ, ROWS, width), bf16),
            vmem((NZ, ROWS, width), bf16),
            vmem((2, REACH + 1, ROWS, width), bf16),
            vmem((2, SEG, ROWS, width), bf16),
            vmem((2, 3, ROWS, width), bf16),
            dma((2, 5, 4, 3)),
            dma((2, 5, 4, 3)),
            dma((2, REACH + 1)),
            dma((2, REACH + 1)),
            dma((2, SEG)),
            dma((2, SEG)),
            dma((2, 3)),
            dma((2,)),
            dma((5,)),
        ],
        compiler_params=pltpu.CompilerParams(collective_id=1, has_side_effects=True),
    )(full, rows, picker)


def prepare_kernel(
    live_ref,
    plan_ref,
    scale_gate_ref,
    scale_up_ref,
    scale_down_ref,
    ids_ref,
    weight_ref,
    tokens_ref,
    cot_ref,
    gate_ref,
    up_ref,
    down_ref,
    w_ref,
    rows_ref,
    pick_ref,
):
    f32 = jnp.float32
    bf16 = jnp.bfloat16
    experts = plan_ref.shape[1]
    count = tokens_ref.shape[0]
    listed = experts * ROWS
    zero = jnp.float32(0.0)

    slot = lax.broadcasted_iota(jnp.int32, (1, count), 1)
    live = slot < live_ref[0]
    odd = slot % 2 == 1
    row = lax.broadcasted_iota(jnp.int32, (listed, count), 0)
    member = jnp.zeros((listed, count), f32)
    weight = jnp.zeros((listed, count), f32)
    ids = ids_ref[...]
    for e in range(experts):
        match = ids == e
        routed = jnp.sum(jnp.where(match, 1.0, 0.0), axis=0, keepdims=True)
        routed = jnp.where(live & (routed > 0.0), 1.0, 0.0)
        weight_sum = jnp.sum(jnp.where(match, weight_ref[...], zero), axis=0, keepdims=True)
        weight = jnp.where(row // ROWS == e, weight_sum, weight)
        split = jnp.where(plan_ref[0, e] == 1, 1.0, 0.0)
        second = routed * jnp.where(odd, split, 0.0)
        member = jnp.where(row // CAP == 2 * e, routed - second, member)
        member = jnp.where(row // CAP == 2 * e + 1, second, member)
    before = lax.broadcasted_iota(jnp.int32, (count, count), 0)
    after = lax.broadcasted_iota(jnp.int32, (count, count), 1)
    ladder = jnp.where(before <= after, 1.0, 0.0).astype(bf16)
    nth = jnp.dot(member.astype(bf16), ladder, preferred_element_type=f32)
    chosen = (member > 0.5) & (nth == (row % CAP + 1).astype(f32))
    chosen = jnp.where(chosen, 1.0, 0.0)
    picker = chosen.astype(bf16)
    pick_ref[...] = picker
    row_weight = jnp.sum(chosen * weight, axis=1, keepdims=True)
    token_rows = jnp.dot(picker, tokens_ref[...], preferred_element_type=f32)
    cot_rows = row_weight * jnp.dot(picker, cot_ref[...], preferred_element_type=f32)
    for e in range(experts):
        rows_ref[e, 0] = token_rows[e * ROWS : (e + 1) * ROWS].astype(bf16)
        rows_ref[e, 1] = cot_rows[e * ROWS : (e + 1) * ROWS].astype(bf16)

    depth = gate_ref.shape[0]
    first = lax.axis_index("dp") * depth
    base = first // BLOCK
    block = (first + lax.broadcasted_iota(jnp.int32, (depth, BLOCK), 0)) // BLOCK - base
    for m, (values, scale) in enumerate(
        ((gate_ref, scale_gate_ref), (up_ref, scale_up_ref), (down_ref, scale_down_ref))
    ):
        most = scale.shape[1] - 1
        for part in range(scale.shape[0]):
            at = pl.ds(part * BLOCK, BLOCK)
            spread = jnp.where(
                block == 0,
                scale[part, base],
                jnp.where(
                    block == 1,
                    scale[part, jnp.minimum(base + 1, most)],
                    scale[part, jnp.minimum(base + 2, most)],
                ),
            )
            w_ref[m, :, at] = (values[:, at].astype(f32) * spread).astype(bf16)


def prepare(tokens, cotangent, route_weight, expert_ids, live, plan, weights, scales):
    count, width = tokens.shape
    experts = plan.shape[1]
    smem = pl.BlockSpec(memory_space=pltpu.SMEM)
    vmem = pl.BlockSpec(memory_space=pltpu.VMEM)
    return pl.pallas_call(
        prepare_kernel,
        out_shape=(
            jax.ShapeDtypeStruct((len(weights),) + weights[0].shape, jnp.bfloat16),
            jax.ShapeDtypeStruct((experts, 2, ROWS, width), jnp.bfloat16),
            jax.ShapeDtypeStruct((experts * ROWS, count), jnp.bfloat16),
        ),
        in_specs=[smem] * 5 + [vmem] * 7,
        out_specs=(vmem,) * 3,
    )(live, plan, *scales, expert_ids.T, route_weight.T, tokens, cotangent, *weights)


def on_device(
    tokens,
    cotangent,
    route_weight,
    expert_ids,
    live_tokens,
    replica_plan,
    w_gate,
    w_up,
    w_down,
    scale_gate,
    scale_up,
    scale_down,
):
    width = tokens.shape[1]
    weights, rows, picker = prepare(
        tokens,
        cotangent,
        route_weight,
        expert_ids,
        live_tokens,
        replica_plan,
        (w_gate, w_up, w_down.T),
        (scale_gate.T, scale_up.T, scale_down),
    )
    full, arrived, _ = gather(weights, rows)
    d_tokens, grad_gate, grad_up, grad_down = layer_and_reduce(
        full.reshape(full.shape[0], -1, full.shape[-1]), arrived.reshape(2, -1, width), picker
    )
    return (d_tokens, grad_gate, grad_up, grad_down.T)


def solution(mesh):
    return jax.shard_map(
        on_device,
        mesh=mesh,
        in_specs=(
            P(("dp", "expert"), None),
            P(("dp", "expert"), None),
            P(("dp", "expert"), None),
            P(("dp", "expert"), None),
            P(("dp", "expert")),
            P(("dp", "expert"), None),
            P("dp", "expert"),
            P("dp", "expert"),
            P("expert", "dp"),
            P(None, "expert"),
            P(None, "expert"),
            P("expert", None),
        ),
        out_specs=(
            P(("dp", "expert"), None),
            P("dp", "expert"),
            P("dp", "expert"),
            P("expert", "dp"),
        ),
        check_vma=False,
    )
```
